32 devices in a mesh: abl: 2 (over y), head: 4 (over x, core), ctx: 4 (over z).
Axes of the slice: x: 2, y: 2, z: 4, core: 2. Of those that a mesh axis runs over, the one named last changes fastest.
Arguments:
- queries: bfloat16 [1024, 6144], P(('abl', 'head', 'ctx')), parts along dimension 0, may hold values from -30 to 30
- keys: bfloat16 [16384, 6144], P(('abl', 'ctx'), 'head'), parts along dimension 0, may hold values from -6 to 6
- values: bfloat16 [16384, 6144], P(('abl', 'ctx'), 'head'), parts along dimension 0, may hold values from -6 to 6
- kept_rows: int32 [128], P(('abl', 'ctx')), parts along dimension 0, may hold values from 0 to 1, as said below
- out_weight: bfloat16 [6144, 6144], P('head'), may hold values from -6 to 6
Outputs:
- projected: bfloat16 [1024, 6144], P(('abl', 'head', 'ctx')), parts along dimension 0
The draws below stay inside these ranges and needn't reach their ends.
There are 2 independent parts, one for each index of `abl`. The reference program is written for one: setup_inputs(seed, part) draws one part's arguments, and reference() takes and returns one part's arrays. A program takes and returns all parts, laid end to end along the dimension named above; an argument that names none is the same for every part. Nothing has to cross between parts.
Inputs may be any that keep to these rules, and one draw needn't show every extreme that they name: `kept_rows`: in every part the first row of each block of 16 consecutive rows is kept.
All inputs are finite; a program needn't handle non-finite values.
Results may differ from the reference program's by a relative error of at most 0.028.
Values may be sent and summed in bfloat16 or wider, within the bound.
No kernel may reach another device: no remote copies, remote signals or barrier semaphores. Data moves between devices by JAX's collectives and lax.ppermute only.
A program may use at most 128 MiB of HBM per device.

```python
import math
import jax
import jax.numpy as jnp
from jax import lax

HEADS = 48
HD = 128
Q_TOK = 512
KV_DEV = 2048
KEPT = 8192
N_CTX = 4


def joint_draw(key):
    key_query, key_key = jax.random.split(key, 2)
    width = HEADS * HD
    query_draw = jnp.clip(jax.random.normal(key_query, (Q_TOK, width), jnp.float32), -6.0, 6.0)
    key_draw = jnp.clip(jax.random.normal(key_key, (KEPT, width), jnp.float32), -6.0, 6.0)
    return (query_draw, key_draw)


def draw_queries(key, part):
    return joint_draw(jax.random.fold_in(key, 7))[0].astype(jnp.bfloat16)


def draw_keys(key, part):
    return joint_draw(jax.random.fold_in(key, 7))[1].astype(jnp.bfloat16)


def draw_kept_rows(key, part):
    row_total = KEPT // 128
    block_rows = KV_DEV // 128
    key_flags, key_block, key_offset = jax.random.split(key, 3)
    flags = (jax.random.randint(key_flags, (row_total,), 0, 4) > 0).astype(jnp.int32)
    position = jnp.arange(row_total)
    dropped_block = jax.random.randint(key_block, (), 0, row_total // block_rows)
    dropped_offset = jax.random.randint(key_offset, (), 1, block_rows)
    dropped = dropped_block * block_rows + dropped_offset
    flags = jnp.where(position == dropped, 0, flags)
    return jnp.where(position % block_rows == 0, 1, flags).astype(jnp.int32)


def shard_levels(stream_key, dims, pieces, least, largest):
    def one(dim, parts):
        heights = jax.random.uniform(jax.random.fold_in(jax.random.fold_in(stream_key, 6), dim), (parts,), jnp.float32, least / len(pieces), largest / len(pieces))
        return jnp.repeat(jnp.exp(heights), dims[dim] // parts).reshape((-1,) + (1,) * (len(dims) - dim - 1))

    loudness = one(*pieces[0])
    for cut in pieces[1:]:
        loudness = loudness * one(*cut)
    return loudness


def gaussian(own_key, dims, deviation, limit, pieces=(), dtype=jnp.bfloat16):
    level = shard_levels(own_key, dims, pieces, -0.22, 0.18) if pieces else 1.0
    array = jax.random.normal(own_key, dims, jnp.float32) * deviation * level
    return jnp.minimum(jnp.maximum(array, -limit), limit).astype(dtype)


def setup_inputs(seed: int = 0, part: int = 0) -> dict:
    key_of = jax.random.split(jax.random.key(seed), 6)
    part_splits = jax.random.split(jax.random.fold_in(key_of[5], part), 6)
    return {
        "queries": draw_queries(jax.random.fold_in(jax.random.fold_in(key_of[5], part), 71), part),
        "keys": draw_keys(jax.random.fold_in(jax.random.fold_in(key_of[5], part), 71), part),
        "values": gaussian(part_splits[2], (KEPT, HEADS * HD), 1.0, 6.0, ((0, 4), (1, 4))),
        "kept_rows": draw_kept_rows(jax.random.fold_in(jax.random.fold_in(key_of[5], part), 71), part),
        "out_weight": gaussian(key_of[4], (HEADS * HD, HEADS * HD), (max(1, HEADS * HD // KEPT)) ** -0.5, 6.0, ((0, 4),)),
    }


def reference(queries, keys, values, kept_rows, out_weight):
    score_scale = 1.0 / math.sqrt(HD)
    query_heads = queries.reshape(Q_TOK, HEADS, HD).astype(jnp.float32)
    key_blocks = keys.reshape(N_CTX, KV_DEV, HEADS, HD)
    value_blocks = values.reshape(N_CTX, KV_DEV, HEADS, HD)
    visible = (jnp.repeat(kept_rows, 128) > 0).reshape(N_CTX, KV_DEV)

    def absorb(carry, block):
        summed, running, normal_sum = carry
        key_block, value_block, seen = block
        scores = jnp.einsum('qhd,khd->hqk', query_heads, key_block.astype(jnp.float32)) * score_scale
        scores = jnp.where(seen[None, None, :], scores, -jnp.inf)
        highest = jnp.maximum(running, lax.optimization_barrier(jnp.max(scores, axis=-1)))
        rescale = jnp.exp(running - highest)
        softened = jnp.exp(scores - highest[..., None])
        normal_sum = normal_sum * rescale + lax.optimization_barrier(jnp.sum(softened, axis=-1))
        rounded = softened.astype(jnp.bfloat16).astype(jnp.float32)
        mixed = jnp.einsum('hqk,khd->hqd', rounded, value_block.astype(jnp.float32))
        summed = summed * rescale[..., None] + mixed
        return ((summed, highest, normal_sum), None)
    starting = (jnp.zeros((HEADS, Q_TOK, HD), jnp.float32), jnp.full((HEADS, Q_TOK), -1e+30, jnp.float32), jnp.zeros((HEADS, Q_TOK), jnp.float32))
    finished, _ = lax.scan(absorb, starting, (key_blocks, value_blocks, visible))
    summed, running, normal_sum = finished
    attended = (summed / normal_sum[..., None]).transpose(1, 0, 2).reshape(Q_TOK, HEADS * HD).astype(jnp.bfloat16)
    return jnp.dot(attended, out_weight, preferred_element_type=jnp.float32).astype(jnp.bfloat16)
```

```python
import functools
import math

import jax
import jax.numpy as jnp
from jax import lax
from jax.experimental import pallas as pl
from jax.experimental.pallas import tpu as pltpu
from jax.sharding import PartitionSpec as P

HD = 128
LANES = 128
ROW = 128
LOW = -1e30
SCALE2 = math.log2(math.e) / math.sqrt(HD)
STEP = 32
CHUNKS = 2
TAILS = 1
VMEM = 56 << 20


def swap(x, axis, size, bit):
    return lax.ppermute(x, axis, [(i, i ^ bit) for i in range(size)])


def split_stats(stats):
    lane = lax.broadcasted_iota(jnp.int32, stats.shape, 1)
    high = stats.astype(jnp.bfloat16)
    rest = stats - high.astype(jnp.float32)
    middle = rest.astype(jnp.bfloat16)
    low = (rest - middle.astype(jnp.float32)).astype(jnp.bfloat16)
    return jnp.where(
        lane < STEP,
        high.astype(jnp.float32),
        jnp.where(lane < 2 * STEP, middle.astype(jnp.float32), low.astype(jnp.float32)),
    ).astype(jnp.bfloat16)


def join_stats(packed):
    x = packed.astype(jnp.float32)
    return x + pltpu.roll(x, LANES - STEP, 1) + pltpu.roll(x, LANES - 2 * STEP, 1)


def attend_body(kept_ref, *refs, pieces, heads, per_step):
    q_refs, (k_ref, v_ref) = refs[:pieces], refs[pieces : pieces + 2]
    o_refs, stat_ref = refs[pieces + 2 : 2 * pieces + 2], refs[-1]
    step = pl.program_id(0)
    keys = k_ref.shape[0]
    rows = q_refs[0].shape[0]
    key_row = lax.broadcasted_iota(jnp.int32, (1, keys), 1) // ROW
    bias = jnp.zeros((1, keys), jnp.float32)
    for j in range(keys // ROW):
        bias = jnp.where(key_row == j, jnp.where(kept_ref[j] > 0, 0.0, LOW), bias)
    lane = lax.broadcasted_iota(jnp.int32, (rows, LANES), 1)

    @pl.when(step == 0)
    def _():
        stat_ref[...] = jnp.zeros_like(stat_ref)

    for i in range(per_step):
        head = step * per_step + i
        columns = slice(i * HD, i * HD + HD)
        k = k_ref[:, columns]
        v = v_ref[:, columns]
        v = jnp.concatenate([v, jnp.ones_like(v)], axis=1)
        for d in range(pieces):
            scores = lax.dot_general(
                q_refs[d][:, columns], k, (((1,), (1,)), ((), ())), preferred_element_type=jnp.float32
            )
            scores = scores + bias
            highest = jnp.max(scores, axis=1, keepdims=True)
            probs = jnp.exp2((scores - highest) * SCALE2)
            both = jnp.dot(probs.astype(jnp.bfloat16), v, preferred_element_type=jnp.float32)
            total = both[:, HD:]
            o_refs[d][:, pl.ds(pl.multiple_of(head * HD, HD), HD)] = (both[:, :HD] / total).astype(jnp.bfloat16)
            stat = highest * SCALE2 + jnp.log2(total)
            stat_ref[d] = jnp.where(lane % STEP == head, stat, stat_ref[d])

    @pl.when(step == pl.num_programs(0) - 1)
    def _():
        for d in range(pieces):
            o_refs[d][:, heads * HD :] = split_stats(stat_ref[d])


def attend(kept, q_pieces, keys, values, first, heads):
    pieces = len(q_pieces)
    rows = q_pieces[0].shape[0]
    count = keys.shape[0]
    per_step = 2 if heads % 2 == 0 and first % 2 == 0 else 1
    width = (heads + 1) * HD
    offset = first // per_step
    return pl.pallas_call(
        functools.partial(attend_body, pieces=pieces, heads=heads, per_step=per_step),
        grid=(heads // per_step,),
        in_specs=[pl.BlockSpec(memory_space=pltpu.SMEM)]
        + [pl.BlockSpec((rows, per_step * HD), lambda h: (0, h))] * pieces
        + [pl.BlockSpec((count, per_step * HD), lambda h: (0, h + offset))] * 2,
        out_specs=[pl.BlockSpec((rows, width), lambda h: (0, 0))] * pieces,
        out_shape=[jax.ShapeDtypeStruct((rows, width), jnp.bfloat16)] * pieces,
        scratch_shapes=[pltpu.VMEM((pieces, rows, LANES), jnp.float32)],
        compiler_params=pltpu.CompilerParams(vmem_limit_bytes=VMEM),
        name="attend",
    )(kept, *q_pieces, keys, values)


def shares(parts, heads):
    stats = [join_stats(part[:, heads * HD :]) for part in parts]
    top = functools.reduce(jnp.maximum, stats)
    weights = [jnp.exp2(stat - top) for stat in stats]
    total = functools.reduce(jnp.add, weights)
    return [w / total for w in weights], top + jnp.log2(total)


def mix(parts, weights, h):
    columns = slice(h * HD, h * HD + HD)
    return functools.reduce(
        jnp.add, [w[:, h : h + 1] * part[:, columns].astype(jnp.float32) for w, part in zip(weights, parts)]
    )


def merge_body(*refs, heads):
    parts = [ref[...] for ref in refs[:-1]]
    weights, total = shares(parts, heads)
    for h in range(heads):
        refs[-1][:, h * HD : h * HD + HD] = mix(parts, weights, h).astype(jnp.bfloat16)
    lane = lax.broadcasted_iota(jnp.int32, total.shape, 1)
    spread = jnp.where(
        lane < STEP, total, jnp.where(lane < 2 * STEP, pltpu.roll(total, STEP, 1), pltpu.roll(total, 2 * STEP, 1))
    )
    refs[-1][:, heads * HD :] = split_stats(spread)


def merge(parts, heads):
    if len(parts) == 1:
        return parts[0]
    return pl.pallas_call(
        functools.partial(merge_body, heads=heads),
        out_shape=jax.ShapeDtypeStruct(parts[0].shape, parts[0].dtype),
        compiler_params=pltpu.CompilerParams(vmem_limit_bytes=VMEM),
        name="merge",
    )(*parts)


def project_body(*refs, counts, heads, group):
    part_refs = refs[: sum(counts)]
    w_ref, keep_ref, send_ref, attended_ref = refs[sum(counts) :]

    @pl.when(pl.program_id(0) == 0)
    def _():
        start, column = 0, 0
        for count, some in zip(counts, heads):
            parts = [ref[...] for ref in part_refs[start : start + count]]
            weights, _ = shares(parts, some)
            for h in range(some):
                attended_ref[:, column : column + HD] = mix(parts, weights, h).astype(jnp.bfloat16)
                column += HD
            start += count

    product = jnp.dot(attended_ref[...], w_ref[...], preferred_element_type=jnp.float32)
    for e in range(product.shape[0] // group):
        target = send_ref if e % 2 else keep_ref
        half = e // 2
        target[half * group : half * group + group, :] = product[e * group : e * group + group, :].astype(jnp.bfloat16)


def project(chunks, heads, weight, group, first, width):
    flat = [part for parts in chunks for part in parts]
    rows = flat[0].shape[0]
    depth = weight.shape[0]
    block = 512
    offset = first // block
    half = jax.ShapeDtypeStruct((rows // 2, width), jnp.bfloat16)
    return pl.pallas_call(
        functools.partial(project_body, counts=[len(parts) for parts in chunks], heads=heads, group=group),
        grid=(width // block,),
        in_specs=[pl.BlockSpec(part.shape, lambda n: (0, 0)) for part in flat]
        + [pl.BlockSpec((depth, block), lambda n: (0, n + offset))],
        out_specs=[pl.BlockSpec((rows // 2, block), lambda n: (0, n))] * 2,
        out_shape=[half, half],
        scratch_shapes=[pltpu.VMEM((rows, depth), jnp.bfloat16)],
        compiler_params=pltpu.CompilerParams(vmem_limit_bytes=VMEM),
        name="project",
    )(*flat, weight)


def shards(queries, keys, values, kept_rows, out_weight, *, n_head, n_ctx):
    local_heads = keys.shape[1] // HD
    group = queries.shape[0]
    rank = lax.axis_index("head")
    edges = [local_heads * i // CHUNKS for i in range(CHUNKS + 1)]
    spans = [(a, b - a) for a, b in zip(edges, edges[1:]) if b > a]

    chunks = []
    for first, heads in spans:
        mine = []
        for e in range(n_head):
            start = (rank ^ e) * (local_heads * HD) + first * HD
            part = lax.dynamic_slice(queries, (0, start), (group, heads * HD))
            mine.append(swap(part, "head", n_head, e) if e else part)
        pieces = {0: jnp.concatenate(mine, axis=0)}
        bit = n_ctx // 2
        while bit:
            pieces.update({d ^ bit: swap(x, "ctx", n_ctx, bit) for d, x in list(pieces.items())})
            bit //= 2
        chunks.append([pieces[d] for d in range(n_ctx)])

    gathered = []
    for (first, heads), q_pieces in zip(spans, chunks):
        partial = attend(kept_rows, q_pieces, keys, values, first, heads)
        waiting = {d: [x] for d, x in enumerate(partial)}
        bit = 1
        while bit < n_ctx:
            for d in reversed(sorted(d for d in waiting if d & bit)):
                waiting[d ^ bit].append(swap(merge(waiting.pop(d), heads), "ctx", n_ctx, bit))
            bit *= 2
        gathered.append(waiting[0])

    width = out_weight.shape[1]
    done = []
    for t in range(TAILS):
        size = width // TAILS
        keep, send = project(gathered, [h for _, h in spans], out_weight, group, t * size, size)
        keep = keep.astype(jnp.float32) + swap(send, "head", n_head, 1).astype(jnp.float32)
        blocks = [keep[i * group : (i + 1) * group] for i in range(n_head // 2)]
        bit = 2
        while bit < n_head:
            sent = blocks[1::2]
            blocks = [
                a + swap(b.astype(jnp.bfloat16), "head", n_head, bit).astype(jnp.float32)
                for a, b in zip(blocks[::2], sent)
            ]
            bit *= 2
        done.append(blocks[0].astype(jnp.bfloat16))
    return jnp.concatenate(done, axis=1)


def solution(mesh):
    placed = (
        P(("abl", "head", "ctx"), None),
        P(("abl", "ctx"), "head"),
        P(("abl", "ctx"), "head"),
        P(("abl", "ctx")),
        P("head", None),
    )
    return jax.shard_map(
        functools.partial(shards, n_head=mesh.shape["head"], n_ctx=mesh.shape["ctx"]),
        mesh=mesh,
        in_specs=placed,
        out_specs=P(("abl", "head", "ctx"), None),
        check_vma=False,
    )
```

```python
import functools
import math

import jax
import jax.numpy as jnp
from jax import lax
from jax.experimental import pallas as pl
from jax.experimental.pallas import tpu as pltpu
from jax.sharding import PartitionSpec as P

HD = 128
LANES = 128
ROW = 128
LOW = -1e30
SCALE2 = math.log2(math.e) / math.sqrt(HD)
STEP = 32
BLOCK = 512
CUTS = 2
TILE = 128
VMEM = 10 << 20


WHOLE = pl.BlockSpec(memory_space=pltpu.VMEM)


def near(x):
    return pltpu.with_memory_space_constraint(x, pltpu.VMEM)


def swap(x, axis, size, bit):
    return lax.ppermute(x, axis, [(i, i ^ bit) for i in range(size)])


def split_stats(stats):
    lane = lax.broadcasted_iota(jnp.int32, stats.shape, 1)
    high = stats.astype(jnp.bfloat16)
    rest = stats - high.astype(jnp.float32)
    middle = rest.astype(jnp.bfloat16)
    low = (rest - middle.astype(jnp.float32)).astype(jnp.bfloat16)
    return jnp.where(
        lane < STEP,
        high.astype(jnp.float32),
        jnp.where(lane < 2 * STEP, middle.astype(jnp.float32), low.astype(jnp.float32)),
    ).astype(jnp.bfloat16)


def join_stats(packed):
    x = packed.astype(jnp.float32)
    return x + pltpu.roll(x, LANES - STEP, 1) + pltpu.roll(x, LANES - 2 * STEP, 1)


def attend_body(kept_ref, *refs, pieces, heads, loads):
    q_refs, (k_ref, v_ref) = refs[:pieces], refs[pieces : pieces + 2]
    o_refs = refs[pieces + 2 : 2 * pieces + 2]
    copies = []
    if loads:
        sources, (k_ref, v_ref, sems) = (k_ref, v_ref), refs[2 * pieces + 2 :]
        for i in range(heads):
            here = pl.ds(i * HD, HD)
            for n, (source, target) in enumerate(zip(sources, (k_ref, v_ref))):
                copies.append(pltpu.make_async_copy(source.at[:, here], target.at[:, here], sems.at[n, i]))
                copies[-1].start()
    keys = k_ref.shape[0]
    rows = q_refs[0].shape[0]
    key_row = lax.broadcasted_iota(jnp.int32, (1, keys), 1) // ROW
    bias = jnp.zeros((1, keys), jnp.float32)
    for j in range(keys // ROW):
        bias = jnp.where(key_row == j, jnp.where(kept_ref[j] > 0, 0.0, LOW), bias)
    together = max(1, min(pieces, TILE // rows))
    tiles = [range(d, min(d + together, pieces)) for d in range(0, pieces, together)]
    work = [(i, tile) for i in range(heads) for tile in tiles]
    lane = lax.broadcasted_iota(jnp.int32, (together * rows, LANES), 1)
    stats = {tile: jnp.zeros((len(tile) * rows, LANES), jnp.float32) for tile in tiles}

    def score(i, tile):
        if loads and tile is tiles[0]:
            copies[2 * i].wait()
            copies[2 * i + 1].wait()
        here = slice(i * HD, i * HD + HD)
        q = [q_refs[d][:, here] for d in tile]
        q = q[0] if len(q) == 1 else jnp.concatenate(q, axis=0)
        return lax.dot_general(q, k_ref[:, here], (((1,), (1,)), ((), ())), preferred_element_type=jnp.float32) + bias

    scores = score(*work[0])
    for at, (i, tile) in enumerate(work):
        following = score(*work[at + 1]) if at + 1 < len(work) else None
        here = slice(i * HD, i * HD + HD)
        v = v_ref[:, here]
        v = jnp.concatenate([v, jnp.ones_like(v)], axis=1)
        highest = jnp.max(scores, axis=1, keepdims=True)
        probs = jnp.exp2((scores - highest) * SCALE2)
        both = jnp.dot(probs.astype(jnp.bfloat16), v, preferred_element_type=jnp.float32)
        total = both[:, HD:]
        mixed = (both[:, :HD] / total).astype(jnp.bfloat16)
        stat = highest * SCALE2 + jnp.log2(total)
        for n, d in enumerate(tile):
            o_refs[d][:, here] = mixed[n * rows : n * rows + rows]
        stats[tile] = jnp.where(lane[: len(tile) * rows] % STEP == i, stat, stats[tile])
        scores = following
    for tile in tiles:
        packed = split_stats(stats[tile])
        for n, d in enumerate(tile):
            o_refs[d][:, heads * HD :] = packed[n * rows : n * rows + rows]


def attend(kept, q_pieces, keys, values, loads):
    pieces = len(q_pieces)
    rows = q_pieces[0].shape[0]
    count = keys.shape[0]
    heads = keys.shape[1] // HD
    source = pl.BlockSpec(memory_space=pltpu.HBM) if loads else WHOLE
    out = [jax.ShapeDtypeStruct((rows, (heads + 1) * HD), jnp.bfloat16)] * pieces
    if loads:
        out += [pltpu.VMEM(keys.shape, keys.dtype), pltpu.VMEM(values.shape, values.dtype)]
    return pl.pallas_call(
        functools.partial(attend_body, pieces=pieces, heads=heads, loads=loads),
        in_specs=[pl.BlockSpec(memory_space=pltpu.SMEM)] + [WHOLE] * pieces + [source] * 2,
        out_specs=[WHOLE] * len(out),
        out_shape=out,
        scratch_shapes=[pltpu.SemaphoreType.DMA((2, heads))] if loads else [],
        compiler_params=pltpu.CompilerParams(vmem_limit_bytes=10 << 20),
        cost_estimate=pl.CostEstimate(
            flops=16 * pieces * rows * count * HD * heads,
            transcendentals=pieces * rows * count * heads,
            bytes_accessed=4 * count * HD * heads,
        ),
        name="attend",
    )(kept, *map(near, q_pieces), keys, values)


def shares(parts, heads):
    stats = [join_stats(part[:, heads * HD :]) for part in parts]
    top = functools.reduce(jnp.maximum, stats)
    weights = [jnp.exp2(stat - top) for stat in stats]
    total = functools.reduce(jnp.add, weights)
    return [w / total for w in weights], top + jnp.log2(total)


def mix(parts, weights, h):
    columns = slice(h * HD, h * HD + HD)
    return functools.reduce(
        jnp.add, [w[:, h : h + 1] * part[:, columns].astype(jnp.float32) for w, part in zip(weights, parts)]
    )


def project_body(*refs, count, heads, group):
    parts = [ref[...] for ref in refs[:count]]
    w_ref, *out_refs = refs[count:]
    weights, _ = shares(parts, heads)
    mixed = [mix(parts, weights, h).astype(jnp.bfloat16) for h in range(heads)]
    attended = mixed[0] if heads == 1 else jnp.concatenate(mixed, axis=1)
    for n in range(0, w_ref.shape[1], BLOCK):
        here = slice(n, n + BLOCK)
        product = jnp.dot(attended, w_ref[:, here], preferred_element_type=jnp.float32)
        for e in range(product.shape[0] // group):
            half = e // 2 * group
            out_refs[e % 2][half : half + group, here] = product[e * group : e * group + group].astype(jnp.bfloat16)


def project(parts, weight, group):
    rows = parts[0].shape[0]
    width = weight.shape[1]
    half = jax.ShapeDtypeStruct((rows // 2, width), jnp.bfloat16)
    return pl.pallas_call(
        functools.partial(project_body, count=len(parts), heads=weight.shape[0] // HD, group=group),
        in_specs=[WHOLE] * (len(parts) + 1),
        out_specs=[WHOLE] * 2,
        out_shape=[half, half],
        compiler_params=pltpu.CompilerParams(vmem_limit_bytes=VMEM),
        cost_estimate=pl.CostEstimate(flops=0, transcendentals=0, bytes_accessed=0),
        name="project",
    )(*map(near, parts), weight)


def exchange(blocks, size, bit):
    out = [t for t in sorted(blocks) if t & bit]
    rows = blocks[0].shape[0]
    got = swap(jnp.concatenate([blocks[t] for t in out], axis=0), "head", size, bit)
    kept = {t: x for t, x in blocks.items() if not t & bit}
    for i, t in enumerate(out):
        kept[t ^ bit] = jnp.concatenate([kept[t ^ bit], got[i * rows : i * rows + rows]], axis=0)
    return kept


def far(x, size):
    return {0: x, size // 2: swap(x, "ctx", size, size // 2)}


def near_side(pieces, size):
    return {1: swap(pieces[0], "ctx", size, 1), **pieces}


def rest(pieces, size):
    pieces = dict(pieces)
    bit = size // 4
    while bit:
        for d, piece in list(pieces.items()):
            if d ^ bit not in pieces:
                pieces[d ^ bit] = swap(piece, "ctx", size, bit)
        bit //= 2
    return pieces


def fold(keep, send, size, top, group):
    bit = 1
    while bit < top:
        wide = send.shape[1] // CUTS
        got = [swap(send[:, n * wide : n * wide + wide], "head", size, bit) for n in range(CUTS)]
        got = jnp.concatenate(got, axis=1)
        total = keep.astype(jnp.float32) + got.astype(jnp.float32)
        bit *= 2
        if bit < top:
            blocks = [total[i : i + group] for i in range(0, total.shape[0], group)]
            keep = jnp.concatenate(blocks[::2], axis=0)
            send = jnp.concatenate(blocks[1::2], axis=0).astype(jnp.bfloat16)
    return total.astype(jnp.bfloat16)


def shards(queries, keys, values, kept_rows, out_weight, *, n_head, n_ctx):
    local_heads = keys.shape[1] // HD
    columns = local_heads * HD
    group = queries.shape[0]
    rank = lax.axis_index("head")
    out_weight = near(out_weight)
    keys = pltpu.with_memory_space_constraint(keys, pltpu.HBM)
    values = pltpu.with_memory_space_constraint(values, pltpu.HBM)
    top = n_head // 2

    blocks = {t: lax.dynamic_slice(queries, (0, (rank ^ t) * columns), (group, columns)) for t in range(n_head)}
    bit = 1
    while bit < top:
        blocks = exchange(blocks, n_head, bit)
        bit *= 2
    own, other = {0: blocks[0]}, {0: swap(blocks[top], "head", n_head, top)}
    own[1] = swap(own[0], "ctx", n_ctx, 1)
    other = near_side(far(other[0], n_ctx), n_ctx)

    def run(side, pieces, need):
        nonlocal kept_rows, keys, values
        loads = not need
        q = [side[d] for d in pieces]
        q, kept_rows, _ = lax.optimization_barrier((q, kept_rows, need))
        out = attend(kept_rows, q, keys, values, loads)
        if loads:
            *out, keys, values = out
            keys, values = near(keys), near(values)
        kept_rows, out = lax.optimization_barrier((kept_rows, out))
        return dict(zip(pieces, out))

    def send(pieces):
        return [x if d == 0 else swap(x, "ctx", n_ctx, d) for d, x in sorted(pieces.items(), reverse=True)]

    low, high = (0, 1), tuple(range(2, n_ctx))
    made = run(own, low, [])
    mine = send(made)
    other_far, gate = lax.optimization_barrier((other[n_ctx // 2], made[0]))
    other[n_ctx // 2] = other_far
    other = rest(other, n_ctx)
    own[0] = lax.optimization_barrier((own[0], gate))[0]
    own[n_ctx // 2] = swap(own[0], "ctx", n_ctx, n_ctx // 2)
    made = run(other, low, [made[0]])
    theirs = send(made)
    own[n_ctx // 2] = lax.optimization_barrier((own[n_ctx // 2], made[0]))[0]
    own = rest(own, n_ctx)
    made = run(other, high, mine)
    theirs += send(made)
    made = run(own, high, theirs[:2])
    mine += send(made)

    theirs, _ = lax.optimization_barrier((theirs, made[2]))
    done = project(theirs, out_weight, group)
    done = fold(*done, n_head, top, group)
    mine, done = lax.optimization_barrier((mine, done))
    other = swap(done, "head", n_head, top)
    done = project(mine, out_weight, group)
    done = fold(*done, n_head, top, group)
    return (done.astype(jnp.float32) + other.astype(jnp.float32)).astype(jnp.bfloat16)


def solution(mesh):
    placed = (
        P(("abl", "head", "ctx"), None),
        P(("abl", "ctx"), "head"),
        P(("abl", "ctx"), "head"),
        P(("abl", "ctx")),
        P("head", None),
    )
    return jax.shard_map(
        functools.partial(shards, n_head=mesh.shape["head"], n_ctx=mesh.shape["ctx"]),
        mesh=mesh,
        in_specs=placed,
        out_specs=P(("abl", "head", "ctx"), None),
        check_vma=False,
    )
```

```python
import functools
import math

import jax
import jax.numpy as jnp
from jax import lax
from jax.experimental import pallas as pl
from jax.experimental.pallas import tpu as pltpu
from jax.sharding import PartitionSpec as P

HD = 128
LANES = 128
ROW = 128
LOW = -1e30
SCALE2 = math.log2(math.e) / math.sqrt(HD)
STEP = 32
BLOCK = 512
CUTS = 2
TILE = 128
VMEM = 10 << 20


WHOLE = pl.BlockSpec(memory_space=pltpu.VMEM)


SMALL = pl.CostEstimate(flops=1, transcendentals=1, bytes_accessed=1)


def near(x):
    return pltpu.with_memory_space_constraint(x, pltpu.VMEM)


def after(x, first):
    return lax.optimization_barrier((x, first))[0]


def swap(x, axis, size, bit):
    return lax.ppermute(x, axis, [(i, i ^ bit) for i in range(size)])


def split_stats(stats):
    lane = lax.broadcasted_iota(jnp.int32, stats.shape, 1)
    high = stats.astype(jnp.bfloat16)
    rest = stats - high.astype(jnp.float32)
    middle = rest.astype(jnp.bfloat16)
    low = (rest - middle.astype(jnp.float32)).astype(jnp.bfloat16)
    return jnp.where(
        lane < STEP,
        high.astype(jnp.float32),
        jnp.where(lane < 2 * STEP, middle.astype(jnp.float32), low.astype(jnp.float32)),
    ).astype(jnp.bfloat16)


def join_stats(packed):
    x = packed.astype(jnp.float32)
    return x + pltpu.roll(x, LANES - STEP, 1) + pltpu.roll(x, LANES - 2 * STEP, 1)


def attend_body(kept_ref, *refs, pieces, heads, loads):
    q_refs, (k_ref, v_ref) = refs[:pieces], refs[pieces : pieces + 2]
    o_refs = refs[pieces + 2 : 2 * pieces + 2]
    copies = []
    if loads:
        sources, (k_ref, v_ref, sems) = (k_ref, v_ref), refs[2 * pieces + 2 :]
        for i in range(heads):
            here = pl.ds(i * HD, HD)
            for n, (source, target) in enumerate(zip(sources, (k_ref, v_ref))):
                copies.append(pltpu.make_async_copy(source.at[:, here], target.at[:, here], sems.at[n, i]))
                copies[-1].start()
    keys = k_ref.shape[0]
    rows = q_refs[0].shape[0]
    key_row = lax.broadcasted_iota(jnp.int32, (1, keys), 1) // ROW
    bias = jnp.zeros((1, keys), jnp.float32)
    for j in range(keys // ROW):
        bias = jnp.where(key_row == j, jnp.where(kept_ref[j] > 0, 0.0, LOW), bias)
    together = max(1, min(pieces, TILE // rows))
    tiles = [range(d, min(d + together, pieces)) for d in range(0, pieces, together)]
    work = [(i, tile) for i in range(heads) for tile in tiles]
    lane = lax.broadcasted_iota(jnp.int32, (together * rows, LANES), 1)
    stats = {tile: jnp.zeros((len(tile) * rows, LANES), jnp.float32) for tile in tiles}

    def score(i, tile):
        if loads and tile is tiles[0]:
            copies[2 * i].wait()
            copies[2 * i + 1].wait()
        here = slice(i * HD, i * HD + HD)
        q = [q_refs[d][:, here] for d in tile]
        q = q[0] if len(q) == 1 else jnp.concatenate(q, axis=0)
        return lax.dot_general(q, k_ref[:, here], (((1,), (1,)), ((), ())), preferred_element_type=jnp.float32) + bias

    scores = score(*work[0])
    for at, (i, tile) in enumerate(work):
        following = score(*work[at + 1]) if at + 1 < len(work) else None
        here = slice(i * HD, i * HD + HD)
        v = v_ref[:, here]
        v = jnp.concatenate([v, jnp.ones_like(v)], axis=1)
        highest = jnp.max(scores, axis=1, keepdims=True)
        probs = jnp.exp2((scores - highest) * SCALE2)
        both = jnp.dot(probs.astype(jnp.bfloat16), v, preferred_element_type=jnp.float32)
        total = both[:, HD:]
        mixed = (both[:, :HD] / total).astype(jnp.bfloat16)
        stat = highest * SCALE2 + jnp.log2(total)
        for n, d in enumerate(tile):
            o_refs[d][:, here] = mixed[n * rows : n * rows + rows]
        stats[tile] = jnp.where(lane[: len(tile) * rows] % STEP == i, stat, stats[tile])
        scores = following
    for tile in tiles:
        packed = split_stats(stats[tile])
        for n, d in enumerate(tile):
            o_refs[d][:, heads * HD :] = packed[n * rows : n * rows + rows]


def attend(kept, q_pieces, keys, values, loads):
    pieces = len(q_pieces)
    rows = q_pieces[0].shape[0]
    count = keys.shape[0]
    heads = keys.shape[1] // HD
    source = pl.BlockSpec(memory_space=pltpu.HBM) if loads else WHOLE
    out = [jax.ShapeDtypeStruct((rows, (heads + 1) * HD), jnp.bfloat16)] * pieces
    if loads:
        out += [pltpu.VMEM(keys.shape, keys.dtype), pltpu.VMEM(values.shape, values.dtype)]
    return pl.pallas_call(
        functools.partial(attend_body, pieces=pieces, heads=heads, loads=loads),
        in_specs=[pl.BlockSpec(memory_space=pltpu.SMEM)] + [WHOLE] * pieces + [source] * 2,
        out_specs=[WHOLE] * len(out),
        out_shape=out,
        scratch_shapes=[pltpu.SemaphoreType.DMA((2, heads))] if loads else [],
        compiler_params=pltpu.CompilerParams(vmem_limit_bytes=10 << 20),
        cost_estimate=pl.CostEstimate(
            flops=16 * pieces * rows * count * HD * heads,
            transcendentals=pieces * rows * count * heads,
            bytes_accessed=4 * count * HD * heads,
        ),
        name="attend",
    )(kept, *map(near, q_pieces), keys, values)


def shares(parts, heads):
    stats = [join_stats(part[:, heads * HD :]) for part in parts]
    top = functools.reduce(jnp.maximum, stats)
    weights = [jnp.exp2(stat - top) for stat in stats]
    total = functools.reduce(jnp.add, weights)
    return [w / total for w in weights], top + jnp.log2(total)


def mix(parts, weights, h):
    columns = slice(h * HD, h * HD + HD)
    return functools.reduce(
        jnp.add, [w[:, h : h + 1] * part[:, columns].astype(jnp.float32) for w, part in zip(weights, parts)]
    )


def merge_body(*refs, heads):
    parts = [ref[...] for ref in refs[:-1]]
    weights, total = shares(parts, heads)
    for h in range(heads):
        refs[-1][:, h * HD : h * HD + HD] = mix(parts, weights, h).astype(jnp.bfloat16)
    lane = lax.broadcasted_iota(jnp.int32, total.shape, 1)
    spread = jnp.where(
        lane < STEP, total, jnp.where(lane < 2 * STEP, pltpu.roll(total, STEP, 1), pltpu.roll(total, 2 * STEP, 1))
    )
    refs[-1][:, heads * HD :] = split_stats(spread)


def merge(parts, heads):
    return pl.pallas_call(
        functools.partial(merge_body, heads=heads),
        in_specs=[WHOLE] * len(parts),
        out_specs=WHOLE,
        out_shape=jax.ShapeDtypeStruct(parts[0].shape, parts[0].dtype),
        compiler_params=pltpu.CompilerParams(vmem_limit_bytes=VMEM),
        cost_estimate=SMALL,
        name="merge",
    )(*map(near, parts))


def project_body(*refs, count, heads, group):
    parts = [ref[...] for ref in refs[:count]]
    w_ref, *out_refs = refs[count:]
    weights, _ = shares(parts, heads)
    mixed = [mix(parts, weights, h).astype(jnp.bfloat16) for h in range(heads)]
    attended = mixed[0] if heads == 1 else jnp.concatenate(mixed, axis=1)
    for n in range(0, w_ref.shape[1], BLOCK):
        here = slice(n, n + BLOCK)
        product = jnp.dot(attended, w_ref[:, here], preferred_element_type=jnp.float32)
        for e in range(product.shape[0] // group):
            half = e // 2 * group
            out_refs[e % 2][half : half + group, here] = product[e * group : e * group + group].astype(jnp.bfloat16)


def project(parts, weight, group):
    rows = parts[0].shape[0]
    width = weight.shape[1]
    half = jax.ShapeDtypeStruct((rows // 2, width), jnp.bfloat16)
    return pl.pallas_call(
        functools.partial(project_body, count=len(parts), heads=weight.shape[0] // HD, group=group),
        in_specs=[WHOLE] * (len(parts) + 1),
        out_specs=[WHOLE] * 2,
        out_shape=[half, half],
        compiler_params=pltpu.CompilerParams(vmem_limit_bytes=VMEM),
        cost_estimate=SMALL,
        name="project",
    )(*map(near, parts), weight)


def exchange(blocks, size, bit):
    out = [t for t in sorted(blocks) if t & bit]
    rows = blocks[0].shape[0]
    got = swap(jnp.concatenate([blocks[t] for t in out], axis=0), "head", size, bit)
    kept = {t: x for t, x in blocks.items() if not t & bit}
    for i, t in enumerate(out):
        kept[t ^ bit] = jnp.concatenate([kept[t ^ bit], got[i * rows : i * rows + rows]], axis=0)
    return kept


def far(x, size):
    return {0: x, size // 2: swap(x, "ctx", size, size // 2)}


def near_side(pieces, size):
    return {1: swap(pieces[0], "ctx", size, 1), **pieces}


def rest(pieces, size):
    pieces = dict(pieces)
    bit = size // 4
    while bit:
        for d, piece in list(pieces.items()):
            if d ^ bit not in pieces:
                pieces[d ^ bit] = swap(piece, "ctx", size, bit)
        bit //= 2
    return pieces


def fold(keep, send, size, top, group):
    bit = 1
    while bit < top:
        wide = send.shape[1] // CUTS
        got = [swap(send[:, n * wide : n * wide + wide], "head", size, bit) for n in range(CUTS)]
        got = jnp.concatenate(got, axis=1)
        total = keep.astype(jnp.float32) + got.astype(jnp.float32)
        bit *= 2
        if bit < top:
            blocks = [total[i : i + group] for i in range(0, total.shape[0], group)]
            keep = jnp.concatenate(blocks[::2], axis=0)
            send = jnp.concatenate(blocks[1::2], axis=0).astype(jnp.bfloat16)
    return total.astype(jnp.bfloat16)


def shards(queries, keys, values, kept_rows, out_weight, *, n_head, n_ctx):
    local_heads = keys.shape[1] // HD
    columns = local_heads * HD
    group = queries.shape[0]
    rank = lax.axis_index("head")
    out_weight = near(out_weight)
    keys = pltpu.with_memory_space_constraint(keys, pltpu.HBM)
    values = pltpu.with_memory_space_constraint(values, pltpu.HBM)
    top = n_head // 2

    blocks = {t: lax.dynamic_slice(queries, (0, (rank ^ t) * columns), (group, columns)) for t in range(n_head)}
    bit = 1
    while bit < top:
        blocks = exchange(blocks, n_head, bit)
        bit *= 2
    far_off = n_ctx // 2
    own, other = {0: blocks[0]}, {0: swap(blocks[top], "head", n_head, top)}
    own[1] = swap(own[0], "ctx", n_ctx, 1)
    others = [d for d in range(n_ctx) if d not in (0, 1, far_off)]
    sides = [own, other]
    parts = [{}, {}]

    def run(pieces, need):
        nonlocal kept_rows, keys, values
        loads = not parts[0]
        q = [sides[side][d] for side, d in pieces]
        q, kept_rows, _ = lax.optimization_barrier((q, kept_rows, need))
        out = attend(kept_rows, q, keys, values, loads)
        if loads:
            *out, keys, values = out
            keys, values = near(keys), near(values)
        kept_rows, out = lax.optimization_barrier((kept_rows, out))
        for (side, d), x in zip(pieces, out):
            parts[side][d] = x

    def send(side, d):
        parts[side][d] = swap(parts[side][d], "ctx", n_ctx, d)

    sides[1] = other = near_side(far(other[0], n_ctx), n_ctx)
    own[far_off] = swap(own[0], "ctx", n_ctx, far_off)
    last = far_off ^ 1

    def passed(side):
        for d in others:
            if d != last:
                send(side, d)
        return [parts[side].pop(far_off), swap(parts[side].pop(last), "ctx", n_ctx, 1)]

    run([(0, 0), (0, 1)], [])
    sides[1] = rest(other, n_ctx)
    run([(1, 0), (1, 1)], [])
    own[far_off] = after(own[far_off], parts[1][0])
    sides[0] = rest(own, n_ctx)
    run([(1, d) for d in [far_off] + others], [])
    for side in (0, 1):
        parts[side][1] = after(parts[side][1], parts[1][far_off])
        send(side, 1)
    relay = passed(1)
    run([(0, d) for d in [far_off] + others], [])
    theirs_through = merge(relay, local_heads)
    parts[1][far_off] = swap(theirs_through, "ctx", n_ctx, far_off)
    through = merge(passed(0), local_heads)
    theirs, mine = list(parts[1].values()), list(parts[0].values())

    theirs, through = lax.optimization_barrier((theirs, through))
    mine.append(swap(through, "ctx", n_ctx, far_off))
    done = fold(*project(theirs, out_weight, group), n_head, top, group)
    mine, done = lax.optimization_barrier((mine, done))
    other = swap(done, "head", n_head, top)
    done = fold(*project(mine, out_weight, group), n_head, top, group)
    return (done.astype(jnp.float32) + other.astype(jnp.float32)).astype(jnp.bfloat16)


def solution(mesh):
    placed = (
        P(("abl", "head", "ctx"), None),
        P(("abl", "ctx"), "head"),
        P(("abl", "ctx"), "head"),
        P(("abl", "ctx")),
        P("head", None),
    )
    return jax.shard_map(
        functools.partial(shards, n_head=mesh.shape["head"], n_ctx=mesh.shape["ctx"]),
        mesh=mesh,
        in_specs=placed,
        out_specs=P(("abl", "head", "ctx"), None),
        check_vma=False,
    )
```

```python
import functools
import math

import jax
import jax.numpy as jnp
from jax import lax
from jax.experimental import pallas as pl
from jax.experimental.pallas import tpu as pltpu
from jax.sharding import PartitionSpec as P

HD = 128
LANES = 128
ROW = 128
LOW = -1e30
SCALE2 = math.log2(math.e) / math.sqrt(HD)
STEP = 32
BLOCK = 1536
CUTS = 2
TILE = 128
VMEM = 10 << 20


WHOLE = pl.BlockSpec(memory_space=pltpu.VMEM)


SMALL = pl.CostEstimate(flops=1, transcendentals=1, bytes_accessed=1)


def near(x):
    return pltpu.with_memory_space_constraint(x, pltpu.VMEM)


def after(x, first):
    return lax.optimization_barrier((x, first))[0]


def swap(x, axis, size, bit):
    return lax.ppermute(x, axis, [(i, i ^ bit) for i in range(size)])


def split_stats(stats):
    lane = lax.broadcasted_iota(jnp.int32, stats.shape, 1)
    high = stats.astype(jnp.bfloat16)
    rest = stats - high.astype(jnp.float32)
    middle = rest.astype(jnp.bfloat16)
    low = (rest - middle.astype(jnp.float32)).astype(jnp.bfloat16)
    return jnp.where(
        lane < STEP,
        high.astype(jnp.float32),
        jnp.where(lane < 2 * STEP, middle.astype(jnp.float32), low.astype(jnp.float32)),
    ).astype(jnp.bfloat16)


def join_stats(packed):
    x = packed.astype(jnp.float32)
    return x + pltpu.roll(x, LANES - STEP, 1) + pltpu.roll(x, LANES - 2 * STEP, 1)


def attend_body(kept_ref, *refs, pieces, heads, loads):
    q_refs, (k_ref, v_ref) = refs[:pieces], refs[pieces : pieces + 2]
    o_refs = refs[pieces + 2 : 2 * pieces + 2]
    copies = []
    if loads:
        sources, (k_ref, v_ref, sems) = (k_ref, v_ref), refs[2 * pieces + 2 :]
        for i in range(heads):
            here = pl.ds(i * HD, HD)
            for n, (source, target) in enumerate(zip(sources, (k_ref, v_ref))):
                copies.append(pltpu.make_async_copy(source.at[:, here], target.at[:, here], sems.at[n, i]))
                copies[-1].start()
    keys = k_ref.shape[0]
    rows = q_refs[0].shape[0]
    key_row = lax.broadcasted_iota(jnp.int32, (1, keys), 1) // ROW
    bias = jnp.zeros((1, keys), jnp.float32)
    for j in range(keys // ROW):
        bias = jnp.where(key_row == j, jnp.where(kept_ref[j] > 0, 0.0, LOW), bias)
    together = max(1, min(pieces, TILE // rows))
    tiles = [range(d, min(d + together, pieces)) for d in range(0, pieces, together)]
    work = [(i, tile) for i in range(heads) for tile in tiles]
    lane = lax.broadcasted_iota(jnp.int32, (together * rows, LANES), 1)
    stats = {tile: jnp.zeros((len(tile) * rows, LANES), jnp.float32) for tile in tiles}

    def score(i, tile):
        if loads and tile is tiles[0]:
            copies[2 * i].wait()
            copies[2 * i + 1].wait()
        here = slice(i * HD, i * HD + HD)
        q = [q_refs[d][:, here] for d in tile]
        q = q[0] if len(q) == 1 else jnp.concatenate(q, axis=0)
        return lax.dot_general(q, k_ref[:, here], (((1,), (1,)), ((), ())), preferred_element_type=jnp.float32) + bias

    scores = score(*work[0])
    for at, (i, tile) in enumerate(work):
        following = score(*work[at + 1]) if at + 1 < len(work) else None
        here = slice(i * HD, i * HD + HD)
        v = v_ref[:, here]
        v = jnp.concatenate([v, jnp.ones_like(v)], axis=1)
        highest = jnp.max(scores, axis=1, keepdims=True)
        probs = jnp.exp2((scores - highest) * SCALE2)
        both = jnp.dot(probs.astype(jnp.bfloat16), v, preferred_element_type=jnp.float32)
        total = both[:, HD:]
        mixed = (both[:, :HD] / total).astype(jnp.bfloat16)
        stat = highest * SCALE2 + jnp.log2(total)
        for n, d in enumerate(tile):
            o_refs[d][:, here] = mixed[n * rows : n * rows + rows]
        stats[tile] = jnp.where(lane[: len(tile) * rows] % STEP == i, stat, stats[tile])
        scores = following
    for tile in tiles:
        packed = split_stats(stats[tile])
        for n, d in enumerate(tile):
            o_refs[d][:, heads * HD :] = packed[n * rows : n * rows + rows]


def attend(kept, q_pieces, keys, values, loads):
    pieces = len(q_pieces)
    rows = q_pieces[0].shape[0]
    count = keys.shape[0]
    heads = keys.shape[1] // HD
    source = pl.BlockSpec(memory_space=pltpu.HBM) if loads else WHOLE
    out = [jax.ShapeDtypeStruct((rows, (heads + 1) * HD), jnp.bfloat16)] * pieces
    if loads:
        out += [pltpu.VMEM(keys.shape, keys.dtype), pltpu.VMEM(values.shape, values.dtype)]
    return pl.pallas_call(
        functools.partial(attend_body, pieces=pieces, heads=heads, loads=loads),
        in_specs=[pl.BlockSpec(memory_space=pltpu.SMEM)] + [WHOLE] * pieces + [source] * 2,
        out_specs=[WHOLE] * len(out),
        out_shape=out,
        scratch_shapes=[pltpu.SemaphoreType.DMA((2, heads))] if loads else [],
        compiler_params=pltpu.CompilerParams(vmem_limit_bytes=10 << 20),
        cost_estimate=pl.CostEstimate(
            flops=16 * pieces * rows * count * HD * heads,
            transcendentals=pieces * rows * count * heads,
            bytes_accessed=4 * count * HD * heads,
        ),
        name="attend",
    )(kept, *map(near, q_pieces), keys, values)


def shares(parts, heads):
    stats = [join_stats(part[:, heads * HD :]) for part in parts]
    top = functools.reduce(jnp.maximum, stats)
    weights = [jnp.exp2(stat - top) for stat in stats]
    total = functools.reduce(jnp.add, weights)
    return [w / total for w in weights], top + jnp.log2(total)


def mix(parts, weights, h):
    columns = slice(h * HD, h * HD + HD)
    return functools.reduce(
        jnp.add, [w[:, h : h + 1] * part[:, columns].astype(jnp.float32) for w, part in zip(weights, parts)]
    )


def merge_body(*refs, heads):
    parts = [ref[...] for ref in refs[:-1]]
    weights, total = shares(parts, heads)
    for h in range(heads):
        refs[-1][:, h * HD : h * HD + HD] = mix(parts, weights, h).astype(jnp.bfloat16)
    lane = lax.broadcasted_iota(jnp.int32, total.shape, 1)
    spread = jnp.where(
        lane < STEP, total, jnp.where(lane < 2 * STEP, pltpu.roll(total, STEP, 1), pltpu.roll(total, 2 * STEP, 1))
    )
    refs[-1][:, heads * HD :] = split_stats(spread)


def merge(parts, heads):
    return pl.pallas_call(
        functools.partial(merge_body, heads=heads),
        in_specs=[WHOLE] * len(parts),
        out_specs=WHOLE,
        out_shape=jax.ShapeDtypeStruct(parts[0].shape, parts[0].dtype),
        compiler_params=pltpu.CompilerParams(vmem_limit_bytes=VMEM),
        cost_estimate=SMALL,
        name="merge",
    )(*map(near, parts))


def project_body(*refs, count, heads, group):
    parts = [ref[...] for ref in refs[:count]]
    w_ref, *out_refs = refs[count:]
    weights, _ = shares(parts, heads)
    mixed = [mix(parts, weights, h).astype(jnp.bfloat16) for h in range(heads)]
    attended = mixed[0] if heads == 1 else jnp.concatenate(mixed, axis=1)
    for n in range(0, w_ref.shape[1], BLOCK):
        here = slice(n, n + BLOCK)
        product = jnp.dot(attended, w_ref[:, here], preferred_element_type=jnp.float32)
        for e in range(product.shape[0] // group):
            half = e // 2 * group
            out_refs[e % 2][half : half + group, here] = product[e * group : e * group + group].astype(jnp.bfloat16)


def project(parts, weight, group):
    rows = parts[0].shape[0]
    width = weight.shape[1]
    half = jax.ShapeDtypeStruct((rows // 2, width), jnp.bfloat16)
    return pl.pallas_call(
        functools.partial(project_body, count=len(parts), heads=weight.shape[0] // HD, group=group),
        in_specs=[WHOLE] * (len(parts) + 1),
        out_specs=[WHOLE] * 2,
        out_shape=[half, half],
        compiler_params=pltpu.CompilerParams(vmem_limit_bytes=VMEM),
        cost_estimate=SMALL,
        name="project",
    )(*map(near, parts), weight)


def exchange(blocks, size, bit):
    out = [t for t in sorted(blocks) if t & bit]
    rows = blocks[0].shape[0]
    got = swap(jnp.concatenate([blocks[t] for t in out], axis=0), "head", size, bit)
    kept = {t: x for t, x in blocks.items() if not t & bit}
    for i, t in enumerate(out):
        kept[t ^ bit] = jnp.concatenate([kept[t ^ bit], got[i * rows : i * rows + rows]], axis=0)
    return kept


def far(x, size):
    return {0: x, size // 2: swap(x, "ctx", size, size // 2)}


def near_side(pieces, size):
    return {1: swap(pieces[0], "ctx", size, 1), **pieces}


def rest(pieces, size):
    pieces = dict(pieces)
    bit = size // 4
    while bit:
        for d, piece in list(pieces.items()):
            if d ^ bit not in pieces:
                pieces[d ^ bit] = swap(piece, "ctx", size, bit)
        bit //= 2
    return pieces


def fold(keep, send, size, top, group):
    bit = 1
    while bit < top:
        wide = send.shape[1] // CUTS
        got = [swap(send[:, n * wide : n * wide + wide], "head", size, bit) for n in range(CUTS)]
        got = jnp.concatenate(got, axis=1)
        total = keep.astype(jnp.float32) + got.astype(jnp.float32)
        bit *= 2
        if bit < top:
            blocks = [total[i : i + group] for i in range(0, total.shape[0], group)]
            keep = jnp.concatenate(blocks[::2], axis=0)
            send = jnp.concatenate(blocks[1::2], axis=0).astype(jnp.bfloat16)
    return total.astype(jnp.bfloat16)


def shards(queries, keys, values, kept_rows, out_weight, *, n_head, n_ctx):
    local_heads = keys.shape[1] // HD
    columns = local_heads * HD
    group = queries.shape[0]
    rank = lax.axis_index("head")
    out_weight = near(out_weight)
    keys = pltpu.with_memory_space_constraint(keys, pltpu.HBM)
    values = pltpu.with_memory_space_constraint(values, pltpu.HBM)
    top = n_head // 2

    blocks = {t: lax.dynamic_slice(queries, (0, (rank ^ t) * columns), (group, columns)) for t in range(n_head)}
    bit = 1
    while bit < top:
        blocks = exchange(blocks, n_head, bit)
        bit *= 2
    far_off = n_ctx // 2
    own, other = {0: blocks[0]}, {0: swap(blocks[top], "head", n_head, top)}
    own[1] = swap(own[0], "ctx", n_ctx, 1)
    others = [d for d in range(n_ctx) if d not in (0, 1, far_off)]
    sides = [own, other]
    parts = [{}, {}]

    def run(pieces, need):
        nonlocal kept_rows, keys, values
        loads = not parts[0]
        q = [sides[side][d] for side, d in pieces]
        q, kept_rows, _ = lax.optimization_barrier((q, kept_rows, need))
        out = attend(kept_rows, q, keys, values, loads)
        if loads:
            *out, keys, values = out
            keys, values = near(keys), near(values)
        kept_rows, out = lax.optimization_barrier((kept_rows, out))
        for (side, d), x in zip(pieces, out):
            parts[side][d] = x

    def send(side, d):
        parts[side][d] = swap(parts[side][d], "ctx", n_ctx, d)

    sides[1] = other = near_side(far(other[0], n_ctx), n_ctx)
    own[far_off] = swap(own[0], "ctx", n_ctx, far_off)
    last = far_off ^ 1

    def passed(side):
        for d in others:
            if d != last:
                send(side, d)
        return [parts[side].pop(far_off), swap(parts[side].pop(last), "ctx", n_ctx, 1)]

    run([(0, 0), (0, 1)], [])
    sides[1] = rest(other, n_ctx)
    run([(1, 0), (1, 1)], [])
    own[far_off] = after(own[far_off], parts[1][0])
    sides[0] = rest(own, n_ctx)
    run([(1, d) for d in [far_off] + others], [])
    for side in (0, 1):
        parts[side][1] = after(parts[side][1], parts[1][far_off])
        send(side, 1)
    relay = passed(1)
    run([(0, d) for d in [far_off] + others], [])
    theirs_through = merge(relay, local_heads)
    parts[1][far_off] = swap(theirs_through, "ctx", n_ctx, far_off)
    through = merge(passed(0), local_heads)
    theirs, mine = list(parts[1].values()), list(parts[0].values())

    theirs, through = lax.optimization_barrier((theirs, through))
    mine.append(swap(through, "ctx", n_ctx, far_off))
    done = fold(*project(theirs, out_weight, group), n_head, top, group)
    other = swap(done, "head", n_head, top)
    mine = after(mine, done)
    done = fold(*project(mine, out_weight, group), n_head, top, group)
    return (done.astype(jnp.float32) + other.astype(jnp.float32)).astype(jnp.bfloat16)


def solution(mesh):
    placed = (
        P(("abl", "head", "ctx"), None),
        P(("abl", "ctx"), "head"),
        P(("abl", "ctx"), "head"),
        P(("abl", "ctx")),
        P("head", None),
    )
    return jax.shard_map(
        functools.partial(shards, n_head=mesh.shape["head"], n_ctx=mesh.shape["ctx"]),
        mesh=mesh,
        in_specs=placed,
        out_specs=P(("abl", "head", "ctx"), None),
        check_vma=False,
    )
```

```python
import functools
import math

import jax
import jax.numpy as jnp
from jax import lax
from jax.experimental import pallas as pl
from jax.experimental.pallas import tpu as pltpu
from jax.sharding import PartitionSpec as P

HD = 128
LANES = 128
ROW = 128
LOW = -1e30
SCALE2 = math.log2(math.e) / math.sqrt(HD)
STEP = 32
BLOCK = 1536
CUTS = 2
TILE = 128
VMEM = 10 << 20


WHOLE = pl.BlockSpec(memory_space=pltpu.VMEM)


SMALL = pl.CostEstimate(flops=1, transcendentals=1, bytes_accessed=1)


def near(x):
    return pltpu.with_memory_space_constraint(x, pltpu.VMEM)


def after(x, first):
    return lax.optimization_barrier((x, first))[0]


def swap(x, axis, size, bit):
    return lax.ppermute(x, axis, [(i, i ^ bit) for i in range(size)])


def split_stats(stats):
    lane = lax.broadcasted_iota(jnp.int32, stats.shape, 1)
    high = stats.astype(jnp.bfloat16)
    rest = stats - high.astype(jnp.float32)
    middle = rest.astype(jnp.bfloat16)
    low = (rest - middle.astype(jnp.float32)).astype(jnp.bfloat16)
    return jnp.where(
        lane < STEP,
        high.astype(jnp.float32),
        jnp.where(lane < 2 * STEP, middle.astype(jnp.float32), low.astype(jnp.float32)),
    ).astype(jnp.bfloat16)


def join_stats(packed):
    x = packed.astype(jnp.float32)
    return x + pltpu.roll(x, LANES - STEP, 1) + pltpu.roll(x, LANES - 2 * STEP, 1)


def attend_body(kept_ref, *refs, pieces, heads, loads):
    q_refs, (k_ref, v_ref) = refs[:pieces], refs[pieces : pieces + 2]
    o_refs = refs[pieces + 2 : 2 * pieces + 2]
    copies = []
    if loads:
        sources, (k_ref, v_ref, sems) = (k_ref, v_ref), refs[2 * pieces + 2 :]
        for i in range(heads):
            here = pl.ds(i * HD, HD)
            for n, (source, target) in enumerate(zip(sources, (k_ref, v_ref))):
                copies.append(pltpu.make_async_copy(source.at[:, here], target.at[:, here], sems.at[n, i]))
                copies[-1].start()
    keys = k_ref.shape[0]
    rows = q_refs[0].shape[0]
    key_row = lax.broadcasted_iota(jnp.int32, (1, keys), 1) // ROW
    bias = jnp.zeros((1, keys), jnp.float32)
    for j in range(keys // ROW):
        bias = jnp.where(key_row == j, jnp.where(kept_ref[j] > 0, 0.0, LOW), bias)
    together = max(1, min(pieces, TILE // rows))
    tiles = [range(d, min(d + together, pieces)) for d in range(0, pieces, together)]
    work = [(i, tile) for i in range(heads) for tile in tiles]
    lane = lax.broadcasted_iota(jnp.int32, (together * rows, LANES), 1)
    stats = {tile: jnp.zeros((len(tile) * rows, LANES), jnp.float32) for tile in tiles}

    def score(i, tile):
        if loads and tile is tiles[0]:
            copies[2 * i].wait()
            copies[2 * i + 1].wait()
        here = slice(i * HD, i * HD + HD)
        q = [q_refs[d][:, here] for d in tile]
        q = q[0] if len(q) == 1 else jnp.concatenate(q, axis=0)
        return lax.dot_general(q, k_ref[:, here], (((1,), (1,)), ((), ())), preferred_element_type=jnp.float32) + bias

    scores = score(*work[0])
    for at, (i, tile) in enumerate(work):
        following = score(*work[at + 1]) if at + 1 < len(work) else None
        here = slice(i * HD, i * HD + HD)
        v = v_ref[:, here]
        v = jnp.concatenate([v, jnp.ones_like(v)], axis=1)
        highest = jnp.max(scores, axis=1, keepdims=True)
        probs = jnp.exp2((scores - highest) * SCALE2)
        both = jnp.dot(probs.astype(jnp.bfloat16), v, preferred_element_type=jnp.float32)
        total = both[:, HD:]
        mixed = (both[:, :HD] / total).astype(jnp.bfloat16)
        stat = highest * SCALE2 + jnp.log2(total)
        for n, d in enumerate(tile):
            o_refs[d][:, here] = mixed[n * rows : n * rows + rows]
        stats[tile] = jnp.where(lane[: len(tile) * rows] % STEP == i, stat, stats[tile])
        scores = following
    for tile in tiles:
        packed = split_stats(stats[tile])
        for n, d in enumerate(tile):
            o_refs[d][:, heads * HD :] = packed[n * rows : n * rows + rows]


def attend(kept, q_pieces, keys, values, loads):
    pieces = len(q_pieces)
    rows = q_pieces[0].shape[0]
    count = keys.shape[0]
    heads = keys.shape[1] // HD
    source = pl.BlockSpec(memory_space=pltpu.HBM) if loads else WHOLE
    out = [jax.ShapeDtypeStruct((rows, (heads + 1) * HD), jnp.bfloat16)] * pieces
    if loads:
        out += [pltpu.VMEM(keys.shape, keys.dtype), pltpu.VMEM(values.shape, values.dtype)]
    return pl.pallas_call(
        functools.partial(attend_body, pieces=pieces, heads=heads, loads=loads),
        in_specs=[pl.BlockSpec(memory_space=pltpu.SMEM)] + [WHOLE] * pieces + [source] * 2,
        out_specs=[WHOLE] * len(out),
        out_shape=out,
        scratch_shapes=[pltpu.SemaphoreType.DMA((2, heads))] if loads else [],
        compiler_params=pltpu.CompilerParams(vmem_limit_bytes=10 << 20),
        cost_estimate=pl.CostEstimate(
            flops=16 * pieces * rows * count * HD * heads,
            transcendentals=pieces * rows * count * heads,
            bytes_accessed=4 * count * HD * heads,
        ),
        name="attend",
    )(kept, *map(near, q_pieces), keys, values)


def shares(parts, heads):
    stats = [join_stats(part[:, heads * HD :]) for part in parts]
    top = functools.reduce(jnp.maximum, stats)
    weights = [jnp.exp2(stat - top) for stat in stats]
    total = functools.reduce(jnp.add, weights)
    return [w / total for w in weights], top + jnp.log2(total)


def mix(parts, weights, h):
    columns = slice(h * HD, h * HD + HD)
    return functools.reduce(
        jnp.add, [w[:, h : h + 1] * part[:, columns].astype(jnp.float32) for w, part in zip(weights, parts)]
    )


def merge_body(*refs, heads):
    parts = [ref[...] for ref in refs[:-1]]
    weights, total = shares(parts, heads)
    for h in range(heads):
        refs[-1][:, h * HD : h * HD + HD] = mix(parts, weights, h).astype(jnp.bfloat16)
    lane = lax.broadcasted_iota(jnp.int32, total.shape, 1)
    spread = jnp.where(
        lane < STEP, total, jnp.where(lane < 2 * STEP, pltpu.roll(total, STEP, 1), pltpu.roll(total, 2 * STEP, 1))
    )
    refs[-1][:, heads * HD :] = split_stats(spread)


def merge(parts, heads):
    return pl.pallas_call(
        functools.partial(merge_body, heads=heads),
        in_specs=[WHOLE] * len(parts),
        out_specs=WHOLE,
        out_shape=jax.ShapeDtypeStruct(parts[0].shape, parts[0].dtype),
        compiler_params=pltpu.CompilerParams(vmem_limit_bytes=VMEM),
        cost_estimate=SMALL,
        name="merge",
    )(*map(near, parts))


def project_body(*refs, count, heads, group):
    parts = [ref[...] for ref in refs[:count]]
    w_ref, *out_refs = refs[count:]
    weights, _ = shares(parts, heads)
    mixed = [mix(parts, weights, h).astype(jnp.bfloat16) for h in range(heads)]
    attended = mixed[0] if heads == 1 else jnp.concatenate(mixed, axis=1)
    for n in range(0, w_ref.shape[1], BLOCK):
        here = slice(n, n + BLOCK)
        product = jnp.dot(attended, w_ref[:, here], preferred_element_type=jnp.float32)
        for e in range(product.shape[0] // group):
            half = e // 2 * group
            out_refs[e % 2][half : half + group, here] = product[e * group : e * group + group].astype(jnp.bfloat16)


def project(parts, weight, group):
    rows = parts[0].shape[0]
    width = weight.shape[1]
    half = jax.ShapeDtypeStruct((rows // 2, width), jnp.bfloat16)
    return pl.pallas_call(
        functools.partial(project_body, count=len(parts), heads=weight.shape[0] // HD, group=group),
        in_specs=[WHOLE] * (len(parts) + 1),
        out_specs=[WHOLE] * 2,
        out_shape=[half, half],
        compiler_params=pltpu.CompilerParams(vmem_limit_bytes=VMEM),
        cost_estimate=SMALL,
        name="project",
    )(*map(near, parts), weight)


def exchange(blocks, size, bit):
    out = [t for t in sorted(blocks) if t & bit]
    rows = blocks[0].shape[0]
    got = swap(jnp.concatenate([blocks[t] for t in out], axis=0), "head", size, bit)
    kept = {t: x for t, x in blocks.items() if not t & bit}
    for i, t in enumerate(out):
        kept[t ^ bit] = jnp.concatenate([kept[t ^ bit], got[i * rows : i * rows + rows]], axis=0)
    return kept


def far(x, size):
    return {0: x, size // 2: swap(x, "ctx", size, size // 2)}


def near_side(pieces, size):
    return {1: swap(pieces[0], "ctx", size, 1), **pieces}


def rest(pieces, size):
    pieces = dict(pieces)
    bit = size // 4
    while bit:
        for d, piece in list(pieces.items()):
            if d ^ bit not in pieces:
                pieces[d ^ bit] = swap(piece, "ctx", size, bit)
        bit //= 2
    return pieces


def fold(keep, send, size, top, group):
    bit = 1
    while bit < top:
        wide = send.shape[1] // CUTS
        got = [swap(send[:, n * wide : n * wide + wide], "head", size, bit) for n in range(CUTS)]
        got = jnp.concatenate(got, axis=1)
        total = keep.astype(jnp.float32) + got.astype(jnp.float32)
        bit *= 2
        if bit < top:
            blocks = [total[i : i + group] for i in range(0, total.shape[0], group)]
            keep = jnp.concatenate(blocks[::2], axis=0)
            send = jnp.concatenate(blocks[1::2], axis=0).astype(jnp.bfloat16)
    return total.astype(jnp.bfloat16)


def shards(queries, keys, values, kept_rows, out_weight, *, n_head, n_ctx):
    local_heads = keys.shape[1] // HD
    columns = local_heads * HD
    group = queries.shape[0]
    rank = lax.axis_index("head")
    out_weight = near(out_weight)
    keys = pltpu.with_memory_space_constraint(keys, pltpu.HBM)
    values = pltpu.with_memory_space_constraint(values, pltpu.HBM)
    top = n_head // 2

    blocks = {t: lax.dynamic_slice(queries, (0, (rank ^ t) * columns), (group, columns)) for t in range(n_head)}
    bit = 1
    while bit < top:
        blocks = exchange(blocks, n_head, bit)
        bit *= 2
    far_off = n_ctx // 2
    own, other = {0: blocks[0]}, {0: swap(blocks[top], "head", n_head, top)}
    own[1] = swap(own[0], "ctx", n_ctx, 1)
    others = [d for d in range(n_ctx) if d not in (0, 1, far_off)]
    sides = [own, other]
    parts = [{}, {}]

    def run(pieces, need):
        nonlocal kept_rows, keys, values
        loads = not parts[0]
        q = [sides[side][d] for side, d in pieces]
        q, kept_rows, _ = lax.optimization_barrier((q, kept_rows, need))
        out = attend(kept_rows, q, keys, values, loads)
        if loads:
            *out, keys, values = out
            keys, values = near(keys), near(values)
        kept_rows, out = lax.optimization_barrier((kept_rows, out))
        for (side, d), x in zip(pieces, out):
            parts[side][d] = x

    def send(side, d):
        parts[side][d] = swap(parts[side][d], "ctx", n_ctx, d)

    sides[1] = other = near_side(far(other[0], n_ctx), n_ctx)
    own[far_off] = swap(own[0], "ctx", n_ctx, far_off)
    last = far_off ^ 1

    def passed(side):
        for d in others:
            if d != last:
                send(side, d)
        return [parts[side].pop(far_off), swap(parts[side].pop(last), "ctx", n_ctx, 1)]

    run([(0, 0), (0, 1)], [])
    sides[1] = rest(other, n_ctx)
    run([(1, 0), (1, 1)], [])
    own[far_off] = after(own[far_off], parts[1][0])
    sides[0] = rest(own, n_ctx)
    run([(1, d) for d in [far_off] + others], [])
    parts[1][1] = after(parts[1][1], parts[1][far_off])
    send(1, 1)
    relay = passed(1)
    run([(0, d) for d in [far_off] + others], [])
    theirs_through = merge(relay, local_heads)
    parts[1][far_off] = swap(theirs_through, "ctx", n_ctx, far_off)
    through = merge(passed(0), local_heads)
    theirs, mine = list(parts[1].values()), list(parts[0].values())

    theirs, through = lax.optimization_barrier((theirs, through))
    mine.append(swap(through, "ctx", n_ctx, far_off))
    done = fold(*project(theirs, out_weight, group), n_head, top, group)
    mine[1] = swap(after(mine[1], done), "ctx", n_ctx, 1)
    other = swap(done, "head", n_head, top)
    mine = after(mine, done)
    done = fold(*project(mine, out_weight, group), n_head, top, group)
    return (done.astype(jnp.float32) + other.astype(jnp.float32)).astype(jnp.bfloat16)


def solution(mesh):
    placed = (
        P(("abl", "head", "ctx"), None),
        P(("abl", "ctx"), "head"),
        P(("abl", "ctx"), "head"),
        P(("abl", "ctx")),
        P("head", None),
    )
    return jax.shard_map(
        functools.partial(shards, n_head=mesh.shape["head"], n_ctx=mesh.shape["ctx"]),
        mesh=mesh,
        in_specs=placed,
        out_specs=P(("abl", "head", "ctx"), None),
        check_vma=False,
    )
```
